32 devices in a mesh: grp: 8 (over z, core), atm: 4 (over y, x).
Axes of the slice: x: 2, y: 2, z: 4, core: 2. Of those that a mesh axis runs over, the one named last changes fastest.
Arguments:
- atoms: float32 [2, 8192, 128], P(None, ('grp', 'atm')), may hold values from -6 to 6
- kinds: int32 [2, 8192], P(None, ('grp', 'atm')), may hold values from 0 to 3
- member: int32 [2, 8192], P(None, ('grp', 'atm')), may hold values from 0 to 7
- targets: float32 [2, 64], replicated, may hold values from -900 to 900
- weights: float32 [128, 128], replicated, may hold values from -0.5 to 0.5
- bias: float32 [128], replicated, may hold values from -0.5 to 0.5
- readout: float32 [4, 128], replicated, may hold values from -0.5 to 0.5
- covariance: float32 [16384, 16384], P('grp', 'atm'), as said below
Outputs:
- posterior: float32 [16384, 16384], P('grp', 'atm')
- weights_out: float32 [128, 128], replicated
The draws below stay inside these ranges and needn't reach their ends.
Inputs may be any that keep to these rules, and one draw needn't show every extreme that they name: `covariance`: symmetric and positive definite.
All inputs are finite; a program needn't handle non-finite values.
Results may differ from the reference program's by a relative error of at most 0.0007.
Values sent between devices are 32-bit elements; how exact they have to be, the bound alone decides.
A program may use at most 128 MiB of HBM per device.

```python
import math
import jax
import jax.numpy as jnp
from jax import lax

FEATURES = 128
PARAMS = 16384
GROUP_LOCAL = 8
GROUPS = 64
GROUP_ATOMS = 1024
ATOMS = 8192
TYPES = 4
STEPS = 2
N_GRP = 8


def draw_covariance(key, part):
    key_couple = jax.random.fold_in(key, 11)
    key_diag = jax.random.fold_in(key, 12)
    uniform_raw = jax.random.uniform(key_couple, (PARAMS, PARAMS), jnp.float32, -1.0, 1.0)
    coupling = (uniform_raw + uniform_raw.T) * (0.3 / math.sqrt(PARAMS))
    diag_values = jnp.exp(jax.random.uniform(key_diag, (PARAMS,), jnp.float32, math.log(0.8), math.log(1.6)))
    position = jnp.arange(PARAMS)
    base = coupling.at[position, position].add(diag_values)
    return base


def plant(entries, own_key, least, largest):
    dims = entries.shape
    place = [jax.random.randint(jax.random.fold_in(own_key, axis), (), 0, dims[axis]) for axis in range(len(dims))]
    entries = entries.at[tuple(place)].set(least)
    longest = dims.index(max(dims))
    place[longest] = (place[longest] + 1) % dims[longest]
    return entries.at[tuple(place)].set(largest)


def block_scale(stream_key, extent, pieces, smallest, largest):
    def one(dim, parts):
        heights = jax.random.uniform(jax.random.fold_in(jax.random.fold_in(stream_key, 6), dim), (parts,), jnp.float32, smallest / len(pieces), largest / len(pieces))
        return jnp.repeat(jnp.exp(heights), extent[dim] // parts).reshape((-1,) + (1,) * (len(extent) - dim - 1))

    level = one(*pieces[0])
    for cut in pieces[1:]:
        level = level * one(*cut)
    return level


def normal_values(stream_key, dims, spread, most, shards=(), held_as=jnp.bfloat16):
    gain = block_scale(stream_key, dims, shards, -0.22, 0.18) if shards else 1.0
    result = jax.random.normal(stream_key, dims, jnp.float32) * spread * gain
    return jnp.minimum(jnp.maximum(result, -most), most).astype(held_as)


def setup_inputs(seed: int = 0) -> dict:
    keys = jax.random.split(jax.random.key(seed), 9)
    return {
        "atoms": normal_values(keys[0], (STEPS, ATOMS, FEATURES), 1.0, 6.0, ((1, 32),), jnp.float32),
        "kinds": plant(jax.random.randint(keys[1], (STEPS, ATOMS), 0, TYPES), jax.random.fold_in(keys[1], 1), 0, TYPES - 1).astype(jnp.int32),
        "member": plant(jax.random.randint(keys[2], (STEPS, ATOMS), 0, GROUP_LOCAL), jax.random.fold_in(keys[2], 1), 0, GROUP_LOCAL - 1).astype(jnp.int32),
        "targets": normal_values(keys[3], (STEPS, GROUPS), 150.0, 900.0, (), jnp.float32),
        "weights": normal_values(keys[4], (FEATURES, FEATURES), FEATURES ** -0.5, 0.5, (), jnp.float32),
        "bias": jnp.clip(jax.random.uniform(keys[5], (FEATURES,), jnp.float32, -0.5, 0.5), -0.5, 0.5),
        "readout": normal_values(keys[6], (TYPES, FEATURES), FEATURES ** -0.5, 0.5, (), jnp.float32),
        "covariance": draw_covariance(jax.random.fold_in(keys[8], 71), 0),
    }


forget_rate = 0.98

def local_terms(atoms, kinds, member, weights, bias, readout):
    precise = lax.Precision.HIGHEST
    preact = jnp.dot(atoms.astype(jnp.float32), weights.astype(jnp.float32), precision=precise, preferred_element_type=jnp.float32) + bias
    hidden = jnp.tanh(preact)
    type_hot = (kinds[:, None] == jnp.arange(readout.shape[0])[None, :]).astype(jnp.float32)
    vectors = jnp.dot(type_hot, readout, precision=precise)
    atom_energy = jnp.sum(hidden * vectors, axis=1)
    slope = (1.0 - hidden * hidden) * vectors
    group_hot = (member[:, None] == jnp.arange(GROUP_LOCAL)[None, :]).astype(jnp.float32)
    energies = jnp.dot(atom_energy, group_hot, precision=precise)
    masked = atoms[:, None, :] * group_hot[:, :, None]
    grads = jnp.einsum('agi,ac->gic', masked, slope, precision=precise)
    return (energies, grads.reshape(GROUP_LOCAL, FEATURES * FEATURES))

def reference(atoms, kinds, member, targets, weights, bias, readout, covariance):
    precise = lax.Precision.HIGHEST
    current = weights
    covar = covariance
    identity = jnp.eye(GROUPS, dtype=jnp.float32)
    for update_idx in range(STEPS):

        def block_terms(inputs, current=current):
            return local_terms(inputs[0], inputs[1], inputs[2], current, bias, readout)
        energies, grads = lax.map(block_terms, (atoms[update_idx].reshape(N_GRP, GROUP_ATOMS, FEATURES), kinds[update_idx].reshape(N_GRP, GROUP_ATOMS), member[update_idx].reshape(N_GRP, GROUP_ATOMS)))
        predicted = energies.reshape(GROUPS)
        jacobian = grads.reshape(GROUPS, PARAMS)
        mismatch = targets[update_idx] - predicted
        gains = jnp.dot(covar, jacobian.T, precision=precise)
        curvature = jnp.dot(jacobian, gains, precision=precise)
        innovation = 0.5 * (curvature + curvature.T) + forget_rate * identity
        factor = jnp.linalg.cholesky(innovation)
        inverse = jax.scipy.linalg.cho_solve((factor, True), identity)
        coefficient = jnp.dot(inverse, mismatch, precision=precise)
        change = jnp.dot(gains, coefficient, precision=precise)
        current = current + change.reshape(FEATURES, FEATURES)
        scaled = jnp.dot(gains, inverse, precision=precise)
        covar = (covar - jnp.dot(scaled, gains.T, precision=precise)) / forget_rate
    return (covar, current)
```

```python
import functools
import jax
import jax.numpy as jnp
from jax import lax
from jax.experimental import pallas as pl
from jax.experimental.pallas import tpu as pltpu
from jax.sharding import PartitionSpec as P

GROUP_LOCAL = 8
STEPS = 2
CORES = 2
LANES = 128

forget_rate = 0.98
precise = lax.Precision.HIGHEST
MESH = pl.DeviceIdType.MESH
VM = pl.BlockSpec(memory_space=pltpu.VMEM)


def local_terms(atoms, kinds, member, weights, bias, readout):
    preact = jnp.dot(atoms, weights, precision=precise, preferred_element_type=jnp.float32) + bias
    hidden = jnp.tanh(preact)
    type_hot = (kinds[:, None] == jnp.arange(readout.shape[0])[None, :]).astype(jnp.float32)
    vectors = jnp.dot(type_hot, readout, precision=precise)
    atom_energy = jnp.sum(hidden * vectors, axis=1)
    slope = (1.0 - hidden * hidden) * vectors
    group_hot = (member[:, None] == jnp.arange(GROUP_LOCAL)[None, :]).astype(jnp.float32)
    energies = jnp.dot(atom_energy, group_hot, precision=precise)
    masked = atoms[:, None, :] * group_hot[:, :, None]
    grads = jnp.einsum("agi,ac->gic", masked, slope, precision=precise)
    return energies, grads.reshape(GROUP_LOCAL, -1)


def push(src, dst, sems, recvs, slot, target):
    copy = pltpu.make_async_remote_copy(
        src_ref=src, dst_ref=dst, send_sem=sems.at[slot], recv_sem=recvs.at[slot],
        device_id=target, device_id_type=MESH,
    )
    copy.start()
    return copy


def greet(targets):
    barrier = pltpu.get_barrier_semaphore()
    for target in targets:
        pl.semaphore_signal(barrier, inc=1, device_id=target, device_id_type=MESH)
    pl.semaphore_wait(barrier, len(targets))


def places(n_grp, n_atm):
    row, col = lax.axis_index("grp"), lax.axis_index("atm")
    n_z = n_grp // CORES
    z, core = row // CORES, lax.rem(row, CORES)
    plane = [lax.rem(col + d, n_atm) for d in range(1, n_atm)]
    column = [lax.rem(z + d, n_z) * CORES + core for d in range(1, n_z)]
    partner = z * CORES + (CORES - 1 - core)
    return row, col, z, core, plane, column, partner


def grads_kernel(n_grp, n_atm, x_ref, out_ref, got, a_s, a_r, b_s, b_r, f_s, f_r):
    row, col, z, core, plane, column, partner = places(n_grp, n_atm)
    greet([{"atm": p} for p in plane] + [{"grp": p} for p in column] + [{"grp": partner}])
    first = [push(x_ref.at[p], got.at[i], a_s, a_r, i, {"atm": p}) for i, p in enumerate(plane)]
    total = x_ref[col]
    for i, copy in enumerate(first):
        copy.wait_recv()
        total = total + got[i]
    out_ref[row] = total
    second = [push(out_ref.at[row], out_ref.at[row], b_s, b_r, i, {"grp": p}) for i, p in enumerate(column)]
    last = [push(out_ref.at[row], out_ref.at[row], f_s, f_r, len(column), {"grp": partner})]
    n_z = n_grp // CORES
    for i, copy in enumerate(second):
        copy.wait_recv()
        origin = lax.rem(z + n_z - (i + 1), n_z) * CORES + core
        last.append(push(out_ref.at[origin], out_ref.at[origin], f_s, f_r, i, {"grp": partner}))
    for copy in last:
        copy.wait_recv()
    for copy in first + second + last:
        copy.wait_send()


def share_grads(x, n_grp, n_atm):
    block = x.shape[1:]
    n_z = n_grp // CORES
    dma = pltpu.SemaphoreType.DMA
    return pl.pallas_call(
        functools.partial(grads_kernel, n_grp, n_atm),
        out_shape=jax.ShapeDtypeStruct((n_grp,) + block, jnp.float32),
        in_specs=[VM], out_specs=VM,
        scratch_shapes=[pltpu.VMEM((n_atm - 1,) + block, jnp.float32)]
        + [dma((n_atm - 1,))] * 2 + [dma((n_z - 1,))] * 2 + [dma((n_z,))] * 2,
        compiler_params=pltpu.CompilerParams(collective_id=0, has_side_effects=True),
        name="share_grads",
    )(x)


def gains_kernel(n_grp, n_atm, half, t_ref, row_ref, col_ref, got, quarter,
                 a_s, a_r, r_s, r_r, b_s, b_r, c_s, c_r, f_s, f_r):
    row, col, z, core, plane, column, partner = places(n_grp, n_atm)
    greet([{"atm": p} for p in plane] + [{"grp": p} for p in column] + [{"grp": partner}])
    first = [push(t_ref.at[p], got.at[i], a_s, a_r, i, {"atm": p}) for i, p in enumerate(plane)]
    total = t_ref[col]
    for i, copy in enumerate(first):
        copy.wait_recv()
        total = total + got[i]
    quarter[z] = total
    row_ref[col] = total
    along = [push(quarter.at[z], quarter.at[z], b_s, b_r, i, {"grp": p}) for i, p in enumerate(column)]
    rows = [push(row_ref.at[col], row_ref.at[col], r_s, r_r, i, {"atm": p}) for i, p in enumerate(plane)]
    for copy in along:
        copy.wait_recv()
    across = [
        push(quarter.at[pl.ds(p * half, half)], col_ref.at[core, col], c_s, c_r, i, {"atm": p})
        for i, p in enumerate(plane)
    ]
    col_ref[core, col] = quarter[pl.ds(col * half, half)]
    last = [push(col_ref.at[core, col], col_ref.at[core, col], f_s, f_r, len(plane), {"grp": partner})]
    for i, copy in enumerate(across):
        copy.wait_recv()
        origin = lax.rem(col + n_atm - (i + 1), n_atm)
        last.append(push(col_ref.at[core, origin], col_ref.at[core, origin], f_s, f_r, i, {"grp": partner}))
    for copy in rows + last:
        copy.wait_recv()
    for copy in first + along + rows + across + last:
        copy.wait_send()


def share_gains(t, n_grp, n_atm):
    _, groups, piece = t.shape
    per_col = n_grp // n_atm
    if n_grp % n_atm or per_col % CORES:
        mine = lax.psum(t, "atm")
        full = lax.all_gather(mine, "grp", axis=0).transpose(2, 0, 1, 3).reshape(groups, -1)
        width = full.shape[1] // n_atm
        return mine, lax.dynamic_slice_in_dim(full, lax.axis_index("atm") * width, width, 1)
    half = per_col // CORES
    n_z = n_grp // CORES
    dma = pltpu.SemaphoreType.DMA
    vm = lambda *lead: pltpu.VMEM(lead + (groups, piece), jnp.float32)
    rows, cols = pl.pallas_call(
        functools.partial(gains_kernel, n_grp, n_atm, half),
        out_shape=(
            jax.ShapeDtypeStruct((n_atm, groups, piece), jnp.float32),
            jax.ShapeDtypeStruct((CORES, n_atm, half, groups, piece), jnp.float32),
        ),
        in_specs=[VM], out_specs=(VM, VM),
        scratch_shapes=[vm(n_atm - 1), vm(n_z)]
        + [dma((n_atm - 1,))] * 4 + [dma((n_z - 1,))] * 2 + [dma((n_atm - 1,))] * 2 + [dma((n_atm,))] * 2,
        compiler_params=pltpu.CompilerParams(collective_id=1, has_side_effects=True),
        name="share_gains",
    )(t)
    return rows, cols.transpose(3, 2, 0, 1, 4).reshape(groups, -1)


def gather_kernel(n_atm, v_ref, out_ref, s, r):
    col = lax.axis_index("atm")
    plane = [lax.rem(col + d, n_atm) for d in range(1, n_atm)]
    greet([{"atm": p} for p in plane])
    copies = [push(v_ref, out_ref.at[col], s, r, i, {"atm": p}) for i, p in enumerate(plane)]
    out_ref[col] = v_ref[...]
    for copy in copies:
        copy.wait()


def gather_atm(v, n_atm, ident):
    return pl.pallas_call(
        functools.partial(gather_kernel, n_atm),
        out_shape=jax.ShapeDtypeStruct((n_atm,) + v.shape, jnp.float32),
        in_specs=[VM], out_specs=VM,
        scratch_shapes=[pltpu.SemaphoreType.DMA((n_atm - 1,))] * 2,
        compiler_params=pltpu.CompilerParams(collective_id=ident, has_side_effects=True),
        name="gather_atm%d" % ident,
    )(v)


def split(value):
    high = value.astype(jnp.bfloat16)
    return high, (value - high.astype(jnp.float32)).astype(jnp.bfloat16)


def terms_kernel(groups, jac_ref, p_ref, out_ref, both):
    @pl.when(pl.program_id(0) == 0)
    def _():
        jac = jac_ref[...]
        high = jac.astype(jnp.bfloat16).astype(jnp.float32)
        both[...] = jnp.concatenate([high, jac - high], axis=0).T.astype(jnp.bfloat16)

    high, low = split(p_ref[...])
    one = jnp.dot(high, both[...], preferred_element_type=jnp.float32)
    two = jnp.dot(low, both[...], preferred_element_type=jnp.float32)
    one = one.T
    out_ref[0] = one[:groups] + one[groups:] + two.T[:groups]


def row_terms(covar, jac, n_atm):
    rows, width = covar.shape
    groups = jac.shape[0]
    piece = rows // n_atm
    tile = min(piece, 256)
    per = piece // tile
    return pl.pallas_call(
        functools.partial(terms_kernel, groups),
        grid=(rows // tile,),
        out_shape=jax.ShapeDtypeStruct((n_atm, groups, piece), jnp.float32),
        in_specs=[
            pl.BlockSpec((groups, width), lambda i: (0, 0)),
            pl.BlockSpec((tile, width), lambda i: (i, 0)),
        ],
        out_specs=pl.BlockSpec((1, groups, tile), lambda i: (i // per, 0, lax.rem(i, per))),
        scratch_shapes=[pltpu.VMEM((width, 2 * groups), jnp.bfloat16)],
        compiler_params=pltpu.CompilerParams(vmem_limit_bytes=48 << 20),
        name="row_terms",
    )(jac, covar)


def update_kernel(scale, left_ref, right_ref, p_ref, out_ref, right):
    @pl.when(pl.program_id(0) == 0)
    def _():
        high, low = split(right_ref[...])
        right[...] = jnp.concatenate([high, high, low], axis=0)

    high, low = split(left_ref[...])
    left = jnp.concatenate([high, low, high], axis=1)
    width = p_ref.shape[1]
    part = min(width, 512)
    for k in range(0, width, part):
        down = jnp.dot(left, right[:, k:k + part], preferred_element_type=jnp.float32)
        out_ref[:, k:k + part] = p_ref[:, k:k + part] * scale - down


def final_update(covar, left, right):
    rows, width = covar.shape
    depth = left.shape[1]
    tile = min(rows, 256)
    return pl.pallas_call(
        functools.partial(update_kernel, 1.0 / forget_rate ** STEPS),
        grid=(rows // tile,),
        out_shape=jax.ShapeDtypeStruct((rows, width), jnp.float32),
        in_specs=[
            pl.BlockSpec((tile, depth), lambda i: (i, 0)),
            pl.BlockSpec((depth, width), lambda i: (0, 0)),
            pl.BlockSpec((tile, width), lambda i: (i, 0)),
        ],
        out_specs=pl.BlockSpec((tile, width), lambda i: (i, 0)),
        scratch_shapes=[pltpu.VMEM((3 * depth, width), jnp.bfloat16)],
        compiler_params=pltpu.CompilerParams(vmem_limit_bytes=48 << 20),
        name="final_update",
    )(left, right, covar)


def body(atoms, kinds, member, targets, weights, bias, readout, covariance):
    n_grp, n_atm = lax.axis_size("grp"), lax.axis_size("atm")
    width = covariance.shape[1]
    groups = GROUP_LOCAL * n_grp
    identity = jnp.eye(groups, dtype=jnp.float32)
    dot = functools.partial(jnp.dot, precision=precise)
    current = weights
    past = []
    for step in range(STEPS):
        energies, partial_value = local_terms(
            atoms[step], kinds[step], member[step], current, bias, readout
        )
        blocks = partial_value.reshape(GROUP_LOCAL, n_atm, width).transpose(1, 0, 2)
        tail = jnp.broadcast_to(energies[None, :, None], (n_atm, GROUP_LOCAL, LANES))
        shared = share_grads(jnp.concatenate([blocks, tail], axis=2), n_grp, n_atm)
        shared = shared.reshape(groups, width + LANES)
        jac = shared[:, :width]
        mismatch = targets[step] - shared[:, width]
        terms = row_terms(covariance, jac, n_atm) * (1.0 / forget_rate ** step)
        for age, (rows_old, cols_old, inverse_old) in enumerate(past):
            small = lax.dot_general(jac, cols_old, (((1,), (1,)), ((), ())), precision=precise)
            small = dot(small, inverse_old) * (1.0 / forget_rate ** (step - age))
            terms = terms - jnp.einsum("xy,nyp->nxp", small, rows_old, precision=precise)
        rows, cols = share_gains(terms, n_grp, n_atm)
        part = lax.dot_general(jac, cols, (((1,), (1,)), ((), ())), precision=precise)
        curvature = jnp.sum(gather_atm(part, n_atm, 2), axis=0)
        innovation = 0.5 * (curvature + curvature.T) + forget_rate * identity
        factor = jnp.linalg.cholesky(innovation)
        inverse = jax.scipy.linalg.cho_solve((factor, True), identity)
        coefficient = dot(inverse, mismatch)
        change = dot(coefficient, cols).reshape(-1, current.shape[1])
        current = current + gather_atm(change, n_atm, 3).reshape(current.shape)
        past.append((rows, cols, inverse))
    left, right = [], []
    for age, (rows, cols, inverse) in enumerate(past):
        scaled = jnp.einsum("nxp,xy->npy", rows, inverse, precision=precise)
        left.append(scaled.reshape(-1, groups) * (1.0 / forget_rate ** (STEPS - age)))
        right.append(cols)
    covar = final_update(covariance, jnp.concatenate(left, axis=1), jnp.concatenate(right, axis=0))
    return (covar, current)


def solution(mesh):
    return jax.shard_map(
        body,
        mesh=mesh,
        in_specs=(
            P(None, ("grp", "atm"), None),
            P(None, ("grp", "atm")),
            P(None, ("grp", "atm")),
            P(),
            P(),
            P(),
            P(),
            P("grp", "atm"),
        ),
        out_specs=(P("grp", "atm"), P()),
        check_vma=False,
    )
```

```python
import functools
import jax
import jax.numpy as jnp
from jax import lax
from jax.experimental import pallas as pl
from jax.experimental.pallas import tpu as pltpu
from jax.sharding import PartitionSpec as P

GROUP_LOCAL = 8
STEPS = 2
CORES = 2
LANES = 128
CHUNKS = 2

forget_rate = 0.98
precise = lax.Precision.HIGHEST
MESH = pl.DeviceIdType.MESH
VM = pl.BlockSpec(memory_space=pltpu.VMEM)


def local_terms(atoms, kinds, member, weights, bias, readout):
    preact = jnp.dot(atoms, weights, precision=precise, preferred_element_type=jnp.float32) + bias
    hidden = jnp.tanh(preact)
    type_hot = (kinds[:, None] == jnp.arange(readout.shape[0])[None, :]).astype(jnp.float32)
    vectors = jnp.dot(type_hot, readout, precision=precise)
    atom_energy = jnp.sum(hidden * vectors, axis=1)
    slope = (1.0 - hidden * hidden) * vectors
    group_hot = (member[:, None] == jnp.arange(GROUP_LOCAL)[None, :]).astype(jnp.float32)
    energies = jnp.dot(atom_energy, group_hot, precision=precise)
    masked = atoms[:, None, :] * group_hot[:, :, None]
    grads = jnp.einsum("agi,ac->gic", masked, slope, precision=precise)
    return energies, grads.reshape(GROUP_LOCAL, -1)


def push(src, dst, sems, recvs, slot, target):
    copy = pltpu.make_async_remote_copy(
        src_ref=src, dst_ref=dst, send_sem=sems.at[slot], recv_sem=recvs.at[slot],
        device_id=target, device_id_type=MESH,
    )
    copy.start()
    return copy


def greet(targets):
    barrier = pltpu.get_barrier_semaphore()
    for target in targets:
        pl.semaphore_signal(barrier, inc=1, device_id=target, device_id_type=MESH)
    pl.semaphore_wait(barrier, len(targets))


def places(n_grp, n_atm):
    row, col = lax.axis_index("grp"), lax.axis_index("atm")
    n_z = n_grp // CORES
    z, core = row // CORES, lax.rem(row, CORES)
    plane = [lax.rem(col + d, n_atm) for d in range(1, n_atm)]
    column = [lax.rem(z + d, n_z) * CORES + core for d in range(1, n_z)]
    partner = z * CORES + (CORES - 1 - core)
    return row, col, z, core, plane, column, partner


def grads_kernel(n_grp, n_atm, x_ref, out_ref, got, a_s, a_r, b_s, b_r, f_s, f_r):
    row, col, z, core, plane, column, partner = places(n_grp, n_atm)
    greet([{"atm": p} for p in plane] + [{"grp": p} for p in column] + [{"grp": partner}])
    n_z = n_grp // CORES
    wide = x_ref.shape[2]
    middle = wide // 2 // LANES * LANES
    cuts = [pl.ds(0, middle), pl.ds(middle, wide - middle)]
    first, second, last = [], [], []
    for k, cut in enumerate(cuts):
        first.append([push(x_ref.at[p, :, cut], got.at[i, :, cut], a_s.at[k], a_r.at[k], i, {"atm": p}) for i, p in enumerate(plane)])
    for k, cut in enumerate(cuts):
        total = x_ref[col, :, cut]
        for i, copy in enumerate(first[k]):
            copy.wait_recv()
            total = total + got[i, :, cut]
        out_ref[row, :, cut] = total
        place = out_ref.at[row, :, cut]
        second.append([push(place, place, b_s.at[k], b_r.at[k], i, {"grp": p}) for i, p in enumerate(column)])
        last.append(push(place, place, f_s.at[k], f_r.at[k], len(column), {"grp": partner}))
    for k, cut in enumerate(cuts):
        for i, copy in enumerate(second[k]):
            copy.wait_recv()
            origin = lax.rem(z + n_z - (i + 1), n_z) * CORES + core
            place = out_ref.at[origin, :, cut]
            last.append(push(place, place, f_s.at[k], f_r.at[k], i, {"grp": partner}))
    for copy in last:
        copy.wait_recv()
    for copy in sum(first + second, last):
        copy.wait_send()


def share_grads(x, n_grp, n_atm):
    block = x.shape[1:]
    n_z = n_grp // CORES
    dma = pltpu.SemaphoreType.DMA
    return pl.pallas_call(
        functools.partial(grads_kernel, n_grp, n_atm),
        out_shape=jax.ShapeDtypeStruct((n_grp,) + block, jnp.float32),
        in_specs=[VM], out_specs=VM,
        scratch_shapes=[pltpu.VMEM((n_atm - 1,) + block, jnp.float32)]
        + [dma((2, n_atm - 1))] * 2 + [dma((2, n_z - 1))] * 2 + [dma((2, n_z))] * 2,
        compiler_params=pltpu.CompilerParams(collective_id=0, has_side_effects=True),
        name="share_grads",
    )(x)


def gains_kernel(n_grp, n_atm, half, t_ref, row_ref, col_ref, got, quarter,
                 a_s, a_r, r_s, r_r, b_s, b_r, c_s, c_r, f_s, f_r):
    row, col, z, core, plane, column, partner = places(n_grp, n_atm)
    greet([{"atm": p} for p in plane] + [{"grp": p} for p in column] + [{"grp": partner}])
    groups = t_ref.shape[1]
    chunk = groups // CHUNKS
    cuts = [pl.ds(k * chunk, chunk) for k in range(CHUNKS)]
    first, along, rows, across, last = [], [], [], [], []
    for k, cut in enumerate(cuts):
        first.append([push(t_ref.at[p, cut], got.at[i, cut], a_s.at[k], a_r.at[k], i, {"atm": p}) for i, p in enumerate(plane)])
    for k, cut in enumerate(cuts):
        total = t_ref[col, cut]
        for i, copy in enumerate(first[k]):
            copy.wait_recv()
            total = total + got[i, cut]
        quarter[z, cut] = total
        row_ref[col, cut] = total
        along.append([push(quarter.at[z, cut], quarter.at[z, cut], b_s.at[k], b_r.at[k], i, {"grp": p}) for i, p in enumerate(column)])
        rows.append([push(row_ref.at[col, cut], row_ref.at[col, cut], r_s.at[k], r_r.at[k], i, {"atm": p}) for i, p in enumerate(plane)])
    for k, cut in enumerate(cuts):
        for copy in along[k]:
            copy.wait_recv()
        across.append([
            push(quarter.at[pl.ds(p * half, half), cut], col_ref.at[core, col, :, cut], c_s.at[k], c_r.at[k], i, {"atm": p})
            for i, p in enumerate(plane)
        ])
        col_ref[core, col, :, cut] = quarter[pl.ds(col * half, half), cut]
        place = col_ref.at[core, col, :, cut]
        last.append([push(place, place, f_s.at[k], f_r.at[k], len(plane), {"grp": partner})])
    for k, cut in enumerate(cuts):
        for i, copy in enumerate(across[k]):
            copy.wait_recv()
            origin = lax.rem(col + n_atm - (i + 1), n_atm)
            place = col_ref.at[core, origin, :, cut]
            last[k].append(push(place, place, f_s.at[k], f_r.at[k], i, {"grp": partner}))
    for group in rows + last:
        for copy in group:
            copy.wait_recv()
    for group in first + along + rows + across + last:
        for copy in group:
            copy.wait_send()


def share_gains(t, n_grp, n_atm):
    _, groups, piece = t.shape
    per_col = n_grp // n_atm
    if n_grp % n_atm or per_col % CORES:
        mine = lax.psum(t, "atm")
        full = lax.all_gather(mine, "grp", axis=0).transpose(2, 0, 1, 3).reshape(groups, -1)
        width = full.shape[1] // n_atm
        return mine, lax.dynamic_slice_in_dim(full, lax.axis_index("atm") * width, width, 1)
    half = per_col // CORES
    n_z = n_grp // CORES
    dma = pltpu.SemaphoreType.DMA
    vm = lambda *lead: pltpu.VMEM(lead + (groups, piece), jnp.float32)
    rows, cols = pl.pallas_call(
        functools.partial(gains_kernel, n_grp, n_atm, half),
        out_shape=(
            jax.ShapeDtypeStruct((n_atm, groups, piece), jnp.float32),
            jax.ShapeDtypeStruct((CORES, n_atm, half, groups, piece), jnp.float32),
        ),
        in_specs=[VM], out_specs=(VM, VM),
        scratch_shapes=[vm(n_atm - 1), vm(n_z)]
        + [dma((CHUNKS, n_atm - 1))] * 4 + [dma((CHUNKS, n_z - 1))] * 2 + [dma((CHUNKS, n_atm - 1))] * 2 + [dma((CHUNKS, n_atm))] * 2,
        compiler_params=pltpu.CompilerParams(collective_id=1, has_side_effects=True),
        name="share_gains",
    )(t)
    return rows, cols.transpose(3, 2, 0, 1, 4).reshape(groups, -1)


def gather_kernel(n_atm, v_ref, out_ref, s, r):
    col = lax.axis_index("atm")
    plane = [lax.rem(col + d, n_atm) for d in range(1, n_atm)]
    greet([{"atm": p} for p in plane])
    copies = [push(v_ref, out_ref.at[col], s, r, i, {"atm": p}) for i, p in enumerate(plane)]
    out_ref[col] = v_ref[...]
    for copy in copies:
        copy.wait()


def gather_atm(v, n_atm, ident):
    return pl.pallas_call(
        functools.partial(gather_kernel, n_atm),
        out_shape=jax.ShapeDtypeStruct((n_atm,) + v.shape, jnp.float32),
        in_specs=[VM], out_specs=VM,
        scratch_shapes=[pltpu.SemaphoreType.DMA((n_atm - 1,))] * 2,
        compiler_params=pltpu.CompilerParams(collective_id=ident, has_side_effects=True),
        name="gather_atm%d" % ident,
    )(v)


def inverse_kernel(parts_ref, out_ref, work):
    size = out_ref.shape[0]
    total = parts_ref[0]
    for k in range(1, parts_ref.shape[0]):
        total = total + parts_ref[k]
    down = lax.broadcasted_iota(jnp.int32, (size, size), 0)
    over = lax.broadcasted_iota(jnp.int32, (size, size), 1)
    work[...] = 0.5 * (total + total.T) + jnp.where(down == over, forget_rate, 0.0)

    def sweep(k, carry):
        full = work[...]
        row = work[pl.ds(k, 1), :]
        column = jnp.sum(jnp.where(over == k, full, 0.0), axis=1, keepdims=True)
        pivot = 1.0 / jnp.sum(jnp.where(over[:1] == k, row, 0.0), axis=1, keepdims=True)
        row_part, col_part = row * pivot, column * pivot
        swept = full - column * row_part
        swept = jnp.where(down == k, row_part, swept)
        swept = jnp.where(over == k, col_part, swept)
        work[...] = jnp.where((down == k) & (over == k), -pivot, swept)
        return carry

    lax.fori_loop(0, size, sweep, 0)
    out_ref[...] = -work[...]


def innovation_inverse(parts):
    size = parts.shape[-1]
    return pl.pallas_call(
        inverse_kernel,
        out_shape=jax.ShapeDtypeStruct((size, size), jnp.float32),
        in_specs=[VM], out_specs=VM,
        scratch_shapes=[pltpu.VMEM((size, size), jnp.float32)],
        name="innovation_inverse",
    )(parts)


def split(value):
    high = value.astype(jnp.bfloat16)
    return high, (value - high.astype(jnp.float32)).astype(jnp.bfloat16)


def terms_kernel(groups, jac_ref, p_ref, out_ref, both):
    @pl.when(pl.program_id(0) == 0)
    def _():
        jac = jac_ref[...]
        high = jac.astype(jnp.bfloat16).astype(jnp.float32)
        both[...] = jnp.concatenate([high, jac - high], axis=0).T.astype(jnp.bfloat16)

    high, low = split(p_ref[...])
    one = jnp.dot(high, both[...], preferred_element_type=jnp.float32)
    two = jnp.dot(low, both[...], preferred_element_type=jnp.float32)
    one = one.T
    out_ref[0] = one[:groups] + one[groups:] + two.T[:groups]


def row_terms(covar, jac, n_atm):
    rows, width = covar.shape
    groups = jac.shape[0]
    piece = rows // n_atm
    tile = min(piece, 256)
    per = piece // tile
    return pl.pallas_call(
        functools.partial(terms_kernel, groups),
        grid=(rows // tile,),
        out_shape=jax.ShapeDtypeStruct((n_atm, groups, piece), jnp.float32),
        in_specs=[
            pl.BlockSpec((groups, width), lambda i: (0, 0)),
            pl.BlockSpec((tile, width), lambda i: (i, 0)),
        ],
        out_specs=pl.BlockSpec((1, groups, tile), lambda i: (i // per, 0, lax.rem(i, per))),
        scratch_shapes=[pltpu.VMEM((width, 2 * groups), jnp.bfloat16)],
        compiler_params=pltpu.CompilerParams(vmem_limit_bytes=48 << 20),
        name="row_terms",
    )(jac, covar)


def update_kernel(scale, left_ref, right_ref, p_ref, out_ref, right):
    @pl.when(pl.program_id(0) == 0)
    def _():
        high, low = split(right_ref[...])
        right[...] = jnp.concatenate([high, high, low], axis=0)

    high, low = split(left_ref[...])
    left = jnp.concatenate([high, low, high], axis=1)
    width = p_ref.shape[1]
    part = min(width, 512)
    for k in range(0, width, part):
        down = jnp.dot(left, right[:, k:k + part], preferred_element_type=jnp.float32)
        out_ref[:, k:k + part] = p_ref[:, k:k + part] * scale - down


def final_update(covar, left, right):
    rows, width = covar.shape
    depth = left.shape[1]
    tile = min(rows, 256)
    return pl.pallas_call(
        functools.partial(update_kernel, 1.0 / forget_rate ** STEPS),
        grid=(rows // tile,),
        out_shape=jax.ShapeDtypeStruct((rows, width), jnp.float32),
        in_specs=[
            pl.BlockSpec((tile, depth), lambda i: (i, 0)),
            pl.BlockSpec((depth, width), lambda i: (0, 0)),
            pl.BlockSpec((tile, width), lambda i: (i, 0)),
        ],
        out_specs=pl.BlockSpec((tile, width), lambda i: (i, 0)),
        scratch_shapes=[pltpu.VMEM((3 * depth, width), jnp.bfloat16)],
        compiler_params=pltpu.CompilerParams(vmem_limit_bytes=48 << 20),
        name="final_update",
    )(left, right, covar)


def body(atoms, kinds, member, targets, weights, bias, readout, covariance):
    n_grp, n_atm = lax.axis_size("grp"), lax.axis_size("atm")
    width = covariance.shape[1]
    groups = GROUP_LOCAL * n_grp
    dot = functools.partial(jnp.dot, precision=precise)
    current = weights
    past = []
    for step in range(STEPS):
        energies, partial_value = local_terms(
            atoms[step], kinds[step], member[step], current, bias, readout
        )
        blocks = partial_value.reshape(GROUP_LOCAL, n_atm, width).transpose(1, 0, 2)
        tail = jnp.broadcast_to(energies[None, :, None], (n_atm, GROUP_LOCAL, LANES))
        shared = share_grads(jnp.concatenate([blocks, tail], axis=2), n_grp, n_atm)
        shared = shared.reshape(groups, width + LANES)
        jac = shared[:, :width]
        mismatch = targets[step] - shared[:, width]
        terms = row_terms(covariance, jac, n_atm) * (1.0 / forget_rate ** step)
        for age, (rows_old, cols_old, inverse_old) in enumerate(past):
            small = lax.dot_general(jac, cols_old, (((1,), (1,)), ((), ())), precision=precise)
            small = dot(small, inverse_old) * (1.0 / forget_rate ** (step - age))
            terms = terms - jnp.einsum("xy,nyp->nxp", small, rows_old, precision=precise)
        rows, cols = share_gains(terms, n_grp, n_atm)
        part = lax.dot_general(jac, cols, (((1,), (1,)), ((), ())), precision=precise)
        inverse = innovation_inverse(gather_atm(part, n_atm, 2))
        coefficient = dot(inverse, mismatch)
        change = dot(coefficient, cols).reshape(-1, current.shape[1])
        current = current + gather_atm(change, n_atm, 3).reshape(current.shape)
        past.append((rows, cols, inverse))
    left, right = [], []
    for age, (rows, cols, inverse) in enumerate(past):
        scaled = jnp.einsum("nxp,xy->npy", rows, inverse, precision=precise)
        left.append(scaled.reshape(-1, groups) * (1.0 / forget_rate ** (STEPS - age)))
        right.append(cols)
    covar = final_update(covariance, jnp.concatenate(left, axis=1), jnp.concatenate(right, axis=0))
    return (covar, current)


def solution(mesh):
    return jax.shard_map(
        body,
        mesh=mesh,
        in_specs=(
            P(None, ("grp", "atm"), None),
            P(None, ("grp", "atm")),
            P(None, ("grp", "atm")),
            P(),
            P(),
            P(),
            P(),
            P("grp", "atm"),
        ),
        out_specs=(P("grp", "atm"), P()),
        check_vma=False,
    )
```
